32 devices in a mesh: dp: 8 (over z, y), tensor: 4 (over x, core).
Axes of the slice: x: 2, y: 2, z: 4, core: 2. Of those that a mesh axis runs over, the one named last changes fastest.
Arguments:
- hidden: bfloat16 [5120, 1152], P(('dp', 'tensor')), may hold values from -6 to 6
- in_gain: bfloat16 [1152], P('dp'), may hold values from 0.25 to 1.75
- w_query: bfloat16 [1152, 1024], P('dp', 'tensor'), may hold values from -0.1875 to 0.1875
- w_key: bfloat16 [1152, 256], P('dp'), may hold values from -0.1875 to 0.1875
- w_value: bfloat16 [1152, 256], P('dp'), may hold values from -0.1875 to 0.1875
- query_gain: bfloat16 [256], P('dp'), may hold values from 0.25 to 1.75
- key_gain: bfloat16 [256], P('dp'), may hold values from 0.25 to 1.75
- w_output: bfloat16 [1024, 1152], P('tensor', 'dp'), may hold values from -0.1875 to 0.1875
- attn_gain: bfloat16 [1152], P('dp'), may hold values from 0.25 to 1.75
- ffn_gain: bfloat16 [1152], P('dp'), may hold values from 0.25 to 1.75
- w_gate: bfloat16 [1152, 6912], P('dp', 'tensor'), may hold values from -0.1875 to 0.1875
- w_up: bfloat16 [1152, 6912], P('dp', 'tensor'), may hold values from -0.1875 to 0.1875
- w_down: bfloat16 [6912, 1152], P('tensor', 'dp'), may hold values from -0.078125 to 0.078125
- out_gain: bfloat16 [1152], P('dp'), may hold values from 0.25 to 1.75
- cotangent: bfloat16 [5120, 1152], P(('dp', 'tensor')), may hold values from -6 to 6
- segment_ids: int32 [5120], P('dp'), may hold values from 0 to 5119, as said below
- positions: int32 [5120], P('dp'), may hold values from 0 to 1999, as said below
Outputs:
- output: bfloat16 [5120, 1152], P(('dp', 'tensor'))
- grad_hidden: float32 [5120, 1152], P(('dp', 'tensor'))
- grad_in_gain: float32 [1152], P('dp')
- grad_w_query: float32 [1152, 1024], P('dp', 'tensor')
- grad_w_key: float32 [1152, 256], P('dp')
- grad_w_value: float32 [1152, 256], P('dp')
- grad_query_gain: float32 [256], P('dp')
- grad_key_gain: float32 [256], P('dp')
- grad_w_output: float32 [1024, 1152], P('tensor', 'dp')
- grad_attn_gain: float32 [1152], P('dp')
- grad_ffn_gain: float32 [1152], P('dp')
- grad_w_gate: float32 [1152, 6912], P('dp', 'tensor')
- grad_w_up: float32 [1152, 6912], P('dp', 'tensor')
- grad_w_down: float32 [6912, 1152], P('tensor', 'dp')
- grad_out_gain: float32 [1152], P('dp')
The draws below stay inside these ranges and needn't reach their ends.
Inputs may be any that keep to these rules, and one draw needn't show every extreme that they name: `segment_ids`: segment ids never fall along the tokens and are equal exactly within a document; a document's id is the index of its first token, except that the document holding the last token has id 5120 - 1; every document holds 200 to 2000 tokens, except that the last may be cut short by the end of the array, and one document holds exactly 2000; documents may run across the bounds of packed sequences. `positions`: the offset of each token from the first token of its document.
All inputs are finite; a program needn't handle non-finite values.
Results may differ from the reference program's by a relative error of at most 0.025.
Values may be sent and summed in bfloat16 or wider, within the bound.
A program may use at most 128 MiB of HBM per device.

```python
import jax
import jax.numpy as jnp
from jax import lax

D = 1152
FF = 6912
H = 4
HD = 256
WINDOW = 512
SEQ = 640
DOC_LEAST = 200
DOC_MOST = 2000
TOKENS = 5120
N_DP = 8
N_TENSOR = 4


def document_layout(key):
    doc_slots = TOKENS // DOC_LEAST + 1
    lengths = jax.random.randint(jax.random.fold_in(key, 11), (doc_slots,), DOC_LEAST, DOC_MOST + 1)
    chosen = jax.random.randint(jax.random.fold_in(key, 12), (), 0, max(TOKENS // DOC_MOST - 1, 1))
    slot_index = jnp.arange(doc_slots, dtype=jnp.int32)
    lengths = jnp.where(slot_index == chosen, DOC_MOST, lengths).astype(jnp.int32)
    ends = jnp.cumsum(lengths)
    starts = ends - lengths
    token_index = jnp.arange(TOKENS, dtype=jnp.int32)
    begin = jnp.max(jnp.where(starts[None, :] <= token_index[:, None], starts[None, :], 0), axis=1)
    finish = jnp.min(jnp.where(ends[None, :] > token_index[:, None], ends[None, :], 4 * TOKENS + 4 * DOC_MOST), axis=1)
    segment = jnp.where(finish >= TOKENS, TOKENS - 1, begin)
    return (segment.astype(jnp.int32), (token_index - begin).astype(jnp.int32))


def draw_segment_ids(key, part):
    return document_layout(key)[0]


def draw_positions(key, part):
    return document_layout(key)[1]


def strengthened(drawn, rng, source, target, shards_of, factor):
    def block_of(axis_at):
        return (jnp.arange(drawn.shape[axis_at]) // (drawn.shape[axis_at] // shards_of)).reshape((-1,) + (1,) * (drawn.ndim - 1 - axis_at))

    one_side = jax.random.permutation(rng, shards_of)[block_of(target)]
    second = (block_of(target) + shards_of // 2) % shards_of
    return jnp.where((block_of(source) == one_side) | (block_of(source) == second), factor * drawn, drawn)


def levels(own_key, dims, shards, smallest, top_value):
    gain = 1.0
    for dim, blocks in shards:
        heights = jax.random.uniform(jax.random.fold_in(jax.random.fold_in(own_key, 6), dim), (blocks,), jnp.float32, smallest / len(shards), top_value / len(shards))
        gain = gain * jnp.repeat(jnp.exp(heights), dims[dim] // blocks).reshape((-1,) + (1,) * (len(dims) - 1 - dim))
    return gain


def gaussian(stream_key, shape, scale, most, split=(), kind=jnp.bfloat16):
    drawn = jax.random.normal(stream_key, shape, jnp.float32) * scale
    if len(split) > 0:
        drawn = levels(stream_key, shape, split, -0.22, 0.18) * drawn
    return jnp.clip(drawn, min=-most, max=most).astype(kind)


def heavy_noise(key, shape, deviation, most, cuts, heavy, held_as=jnp.bfloat16):
    values = deviation * jax.random.normal(key, shape, jnp.float32)
    if cuts:
        values = values * levels(key, shape, cuts, -0.22, 0.18)
    return jnp.clip(strengthened(values, jax.random.fold_in(key, 3), *heavy), -most, most).astype(held_as)


def setup_inputs(seed: int = 0) -> dict:
    seeds = jax.random.split(jax.random.key(seed), 18)
    hidden = heavy_noise(seeds[0], (TOKENS, D), 1.0, 6.0, ((0, 32),), (0, 1, 32, 2.75))
    in_gain = jnp.clip(1.0 + 0.15 * jax.random.normal(seeds[1], (D,), jnp.float32), 0.25, 1.75).astype(jnp.bfloat16)
    w_query = gaussian(seeds[2], (D, H * HD), D ** -0.5, 0.1875, ((0, 8), (1, 4)))
    w_key = gaussian(seeds[3], (D, HD), D ** -0.5, 0.1875, ((0, 8),))
    w_value = gaussian(seeds[4], (D, HD), D ** -0.5, 0.1875, ((0, 8),))
    query_gain = jnp.clip(1.0 + 0.15 * jax.random.normal(seeds[5], (HD,), jnp.float32), 0.25, 1.75).astype(jnp.bfloat16)
    key_gain = jnp.clip(1.0 + 0.15 * jax.random.normal(seeds[6], (HD,), jnp.float32), 0.25, 1.75).astype(jnp.bfloat16)
    w_output = gaussian(seeds[7], (H * HD, D), (H * HD) ** -0.5, 0.1875, ((0, 4), (1, 8)))
    attn_gain = jnp.clip(1.0 + 0.15 * jax.random.normal(seeds[8], (D,), jnp.float32), 0.25, 1.75).astype(jnp.bfloat16)
    ffn_gain = jnp.clip(1.0 + 0.15 * jax.random.normal(seeds[9], (D,), jnp.float32), 0.25, 1.75).astype(jnp.bfloat16)
    w_gate = gaussian(seeds[10], (D, FF), D ** -0.5, 0.1875, ((0, 8), (1, 4)))
    w_up = gaussian(seeds[11], (D, FF), D ** -0.5, 0.1875, ((0, 8), (1, 4)))
    w_down = gaussian(seeds[12], (FF, D), FF ** -0.5, 0.078125, ((0, 4), (1, 8)))
    out_gain = jnp.clip(1.0 + 0.15 * jax.random.normal(seeds[13], (D,), jnp.float32), 0.25, 1.75).astype(jnp.bfloat16)
    cotangent = heavy_noise(seeds[14], (TOKENS, D), 1.0, 6.0, ((0, 32),), (0, 1, 32, 2.75))
    segment_ids = draw_segment_ids(jax.random.fold_in(seeds[17], 71), 0)
    positions = draw_positions(jax.random.fold_in(seeds[17], 71), 0)
    return {"hidden": hidden, "in_gain": in_gain, "w_query": w_query, "w_key": w_key, "w_value": w_value, "query_gain": query_gain, "key_gain": key_gain, "w_output": w_output, "attn_gain": attn_gain, "ffn_gain": ffn_gain, "w_gate": w_gate, "w_up": w_up, "w_down": w_down, "out_gain": out_gain, "cotangent": cotangent, "segment_ids": segment_ids, "positions": positions}


EPSILON = 1e-06
ROPE_BASE = 10000.0

def rms_scale(values):
    return lax.rsqrt(lax.optimization_barrier(jnp.mean(values * values, axis=-1, keepdims=True)) + EPSILON)

def apply_norm(values, gain_vec):
    return values * rms_scale(values) * gain_vec.astype(jnp.float32)

def norm_back(values, gain_vec, upstream):
    factor = rms_scale(values)
    unit_rows = values * factor
    scaled = upstream * gain_vec.astype(jnp.float32)
    grad_values = factor * (scaled - unit_rows * lax.optimization_barrier(jnp.mean(scaled * unit_rows, axis=-1, keepdims=True)))
    return (grad_values, upstream * unit_rows)

def rotary_tables(token_pos, width):
    steps_half = jnp.arange(width // 2, dtype=jnp.float32)
    frequency = ROPE_BASE ** (-2.0 * steps_half / width)
    angles = token_pos.astype(jnp.float32)[:, None] * frequency[None, :]
    return (jnp.cos(angles), jnp.sin(angles))

def rotate(values, cosine, sine_table):
    half_width = values.shape[-1] // 2
    first_half = values[..., :half_width]
    second = values[..., half_width:]
    return jnp.concatenate([first_half * cosine - second * sine_table, second * cosine + first_half * sine_table], axis=-1)

def window_mask(seq_ids):
    length_seq = seq_ids.shape[0]
    token_index = jnp.arange(length_seq, dtype=jnp.int32)
    behind = token_index[:, None] - token_index[None, :]
    return (seq_ids[:, None] == seq_ids[None, :]) & (behind >= 0) & (behind < WINDOW)

def gelu_tanh(values):
    return jax.nn.gelu(values, approximate=True)

def round_low(values):
    return lax.optimization_barrier(values.astype(jnp.bfloat16)).astype(jnp.float32)

def token_partials(term):
    blocks = term.reshape(N_TENSOR, SEQ // N_TENSOR, term.shape[-1])
    return lax.optimization_barrier(jnp.sum(round_low(lax.optimization_barrier(jnp.sum(blocks, axis=1))), axis=0))

def head_partials(term):
    groups = term.reshape(SEQ, N_TENSOR, H // N_TENSOR, HD)
    return lax.optimization_barrier(jnp.sum(round_low(lax.optimization_barrier(jnp.sum(groups, axis=(0, 2)))), axis=0))

def reference(hidden, in_gain, w_query, w_key, w_value, query_gain, key_gain, w_output, attn_gain, ffn_gain, w_gate, w_up, w_down, out_gain, cotangent, segment_ids, positions):
    factor = HD ** (-0.5)

    def one_sequence(totals, inputs):
        rows_in, rows_cot, seq_ids, seq_pos = inputs
        hidden_f = rows_in.astype(jnp.float32)
        normed_in = apply_norm(hidden_f, in_gain).astype(jnp.bfloat16)
        query_raw = jnp.dot(normed_in, w_query, preferred_element_type=jnp.float32).reshape(SEQ, H, HD)
        key_raw = jnp.dot(normed_in, w_key, preferred_element_type=jnp.float32)
        value_rows = jnp.dot(normed_in, w_value, preferred_element_type=jnp.float32).astype(jnp.bfloat16)
        cosine, sine_table = rotary_tables(seq_pos, HD)
        query_rot = rotate(apply_norm(query_raw, query_gain), cosine[:, None, :], sine_table[:, None, :]).astype(jnp.bfloat16)
        key_rot = rotate(apply_norm(key_raw, key_gain), cosine, sine_table).astype(jnp.bfloat16)
        allowed = window_mask(seq_ids)[None]
        scores = jnp.einsum('qhd,kd->hqk', query_rot.astype(jnp.float32), key_rot.astype(jnp.float32)) * factor
        log_total = jnp.log(lax.optimization_barrier(jnp.sum(jnp.where(allowed, jnp.exp(scores), 0.0), axis=-1, keepdims=True)))
        probs = jnp.where(allowed, jnp.exp(scores - log_total), 0.0)
        probs_low = probs.astype(jnp.bfloat16)
        context = jnp.einsum('hqk,kd->qhd', probs_low.astype(jnp.float32), value_rows.astype(jnp.float32))
        context = context.reshape(SEQ, H * HD).astype(jnp.bfloat16)
        attn_rows = jnp.dot(context, w_output, preferred_element_type=jnp.float32)
        residual = hidden_f + apply_norm(attn_rows, attn_gain)
        ffn_in = apply_norm(residual, ffn_gain).astype(jnp.bfloat16)
        gate_pre = jnp.dot(ffn_in, w_gate, preferred_element_type=jnp.float32)
        up_pre = jnp.dot(ffn_in, w_up, preferred_element_type=jnp.float32)
        gelu_values, gelu_back = jax.vjp(gelu_tanh, gate_pre)
        mixed = (gelu_values * up_pre).astype(jnp.bfloat16)
        down_rows = jnp.dot(mixed, w_down, preferred_element_type=jnp.float32)
        out_rows = (residual + apply_norm(down_rows, out_gain)).astype(jnp.bfloat16)
        cot_f = rows_cot.astype(jnp.float32)
        grad_down, term_out = norm_back(down_rows, out_gain, cot_f)
        down_low = grad_down.astype(jnp.bfloat16)
        grad_wd = jnp.dot(mixed.T, down_low, preferred_element_type=jnp.float32)
        grad_mixed = jnp.dot(down_low, w_down.T, preferred_element_type=jnp.float32)
        gate_low = gelu_back(grad_mixed * up_pre)[0].astype(jnp.bfloat16)
        up_low = (grad_mixed * gelu_values).astype(jnp.bfloat16)
        grad_wg = jnp.dot(ffn_in.T, gate_low, preferred_element_type=jnp.float32)
        grad_wu = jnp.dot(ffn_in.T, up_low, preferred_element_type=jnp.float32)
        ffn_back = jnp.dot(gate_low, w_gate.T, preferred_element_type=jnp.float32) + jnp.dot(up_low, w_up.T, preferred_element_type=jnp.float32)
        resid_norm, term_ffn = norm_back(residual, ffn_gain, ffn_back)
        grad_residual = cot_f + resid_norm
        grad_attn, term_attn = norm_back(attn_rows, attn_gain, grad_residual)
        attn_low = grad_attn.astype(jnp.bfloat16)
        grad_wo = jnp.dot(context.T, attn_low, preferred_element_type=jnp.float32)
        grad_context = jnp.dot(attn_low, w_output.T, preferred_element_type=jnp.float32).astype(jnp.bfloat16)
        grad_context = grad_context.reshape(SEQ, H, HD).astype(jnp.float32)
        grad_probs = jnp.einsum('qhd,kd->hqk', grad_context, value_rows.astype(jnp.float32))
        delta = lax.optimization_barrier(jnp.sum(probs * grad_probs, axis=-1, keepdims=True))
        grad_scores = (probs * (grad_probs - delta) * factor).astype(jnp.bfloat16).astype(jnp.float32)
        value_heads = jnp.einsum('hqk,qhd->khd', probs_low.astype(jnp.float32), grad_context).astype(jnp.bfloat16)
        grad_qrot = jnp.einsum('hqk,kd->qhd', grad_scores, key_rot.astype(jnp.float32))
        grad_kheads = jnp.einsum('hqk,qhd->khd', grad_scores, query_rot.astype(jnp.float32))
        grad_qraw, term_qgain = norm_back(query_raw, query_gain, rotate(grad_qrot, cosine[:, None, :], -sine_table[:, None, :]))
        grad_kraw, term_kgain = norm_back(key_raw[:, None, :], key_gain, rotate(grad_kheads, cosine[:, None, :], -sine_table[:, None, :]))
        query_low = grad_qraw.astype(jnp.bfloat16).reshape(SEQ, H * HD)
        key_low = grad_kraw.astype(jnp.bfloat16).astype(jnp.float32)
        value_low = value_heads.astype(jnp.float32)
        normed_f = normed_in.astype(jnp.float32)
        grad_wq = jnp.dot(normed_in.T, query_low, preferred_element_type=jnp.float32)
        key_groups = key_low.reshape(SEQ, N_TENSOR, H // N_TENSOR, HD)
        value_groups = value_low.reshape(SEQ, N_TENSOR, H // N_TENSOR, HD)
        grad_wk = lax.optimization_barrier(jnp.sum(round_low(jnp.einsum('sd,sghe->gde', normed_f, key_groups)), axis=0))
        grad_wv = lax.optimization_barrier(jnp.sum(round_low(jnp.einsum('sd,sghe->gde', normed_f, value_groups)), axis=0))
        attn_back = jnp.dot(query_low, w_query.T, preferred_element_type=jnp.float32)
        attn_back = attn_back + jnp.einsum('she,de->sd', key_low, w_key.astype(jnp.float32))
        attn_back = attn_back + jnp.einsum('she,de->sd', value_low, w_value.astype(jnp.float32))
        in_norm, term_in = norm_back(hidden_f, in_gain, attn_back)
        grad_rows = grad_residual + in_norm
        terms = (token_partials(term_in), round_low(grad_wq), grad_wk, grad_wv, head_partials(term_qgain), head_partials(term_kgain), round_low(grad_wo), token_partials(term_attn), token_partials(term_ffn), round_low(grad_wg), round_low(grad_wu), round_low(grad_wd), token_partials(term_out))
        updated = tuple((running + fresh for running, fresh in zip(totals, terms)))
        return (updated, (out_rows, grad_rows))
    shapes = ((D,), (D, H * HD), (D, HD), (D, HD), (HD,), (HD,), (H * HD, D), (D,), (D,), (D, FF), (D, FF), (FF, D), (D,))
    start_totals = tuple((jnp.zeros(shape_one, jnp.float32) for shape_one in shapes))
    inputs = (hidden.reshape(N_DP, SEQ, D), cotangent.reshape(N_DP, SEQ, D), segment_ids.reshape(N_DP, SEQ), positions.reshape(N_DP, SEQ))
    totals, stacked = lax.scan(one_sequence, start_totals, inputs)
    output = stacked[0].reshape(TOKENS, D)
    grad_hidden = stacked[1].reshape(TOKENS, D)
    return (output, grad_hidden, totals[0], totals[1], totals[2], totals[3], totals[4], totals[5], totals[6], totals[7], totals[8], totals[9], totals[10], totals[11], totals[12])
```

```python
import functools

import jax
import jax.numpy as jnp
from jax import lax
from jax.experimental import pallas as pl
from jax.experimental.pallas import tpu as pltpu
from jax.sharding import PartitionSpec as P

HD = 256
WINDOW = 512


EPSILON = 1e-06
ROPE_BASE = 10000.0


def rms_scale(values):
    return lax.rsqrt(jnp.mean(values * values, axis=-1, keepdims=True) + EPSILON)


def apply_norm(values, gain_vec):
    return values * rms_scale(values) * gain_vec.astype(jnp.float32)


def norm_back(values, gain_vec, upstream):
    factor = rms_scale(values)
    unit_rows = values * factor
    scaled = upstream * gain_vec.astype(jnp.float32)
    grad_values = factor * (
        scaled - unit_rows * jnp.mean(scaled * unit_rows, axis=-1, keepdims=True)
    )
    return (grad_values, upstream * unit_rows)


def rotary_tables(token_pos, width):
    steps_half = jnp.arange(width // 2, dtype=jnp.float32)
    frequency = ROPE_BASE ** (-2.0 * steps_half / width)
    angles = token_pos.astype(jnp.float32)[:, None] * frequency[None, :]
    return (jnp.cos(angles), jnp.sin(angles))


def rotate(values, cosine, sine_table):
    half_width = values.shape[-1] // 2
    first_half = values[..., :half_width]
    second = values[..., half_width:]
    return jnp.concatenate(
        [first_half * cosine - second * sine_table, second * cosine + first_half * sine_table],
        axis=-1,
    )


def window_mask(seq_ids):
    length_seq = seq_ids.shape[0]
    token_index = jnp.arange(length_seq, dtype=jnp.int32)
    behind = token_index[:, None] - token_index[None, :]
    return (seq_ids[:, None] == seq_ids[None, :]) & (behind >= 0) & (behind < WINDOW)


def gelu_tanh(values):
    return jax.nn.gelu(values, approximate=True)


def contract_rows(left, right):
    return lax.dot_general(
        left, right, (((0,), (0,)), ((), ())), preferred_element_type=jnp.float32
    )


def contract_cols(left, right):
    return lax.dot_general(
        left, right, (((1,), (1,)), ((), ())), preferred_element_type=jnp.float32
    )


MESH = pl.DeviceIdType.MESH
LANES = 128
SUBLANES = 16


def pieces_of(shapes, wanted):
    pieces = []
    for index, (rows, _) in enumerate(shapes):
        cuts = wanted if rows % (wanted * SUBLANES) == 0 else 1
        size = rows // cuts
        pieces.extend((index, cut * size, size) for cut in range(cuts))
    return pieces


def place_of(axis, n):
    me = lax.axis_index(axis)
    line = me // 2
    side = me - 2 * line
    return me, line, side, 2 * line + 1 - side, n // 2


def greet(partners):
    barrier = pltpu.get_barrier_semaphore()
    for name, index in partners:
        pl.semaphore_signal(barrier, inc=1, device_id={name: index}, device_id_type=MESH)
    pl.semaphore_wait(barrier, len(partners))


def remote(axis, target, src, dst, send, recv):
    return pltpu.make_async_remote_copy(
        src_ref=src,
        dst_ref=dst,
        send_sem=send,
        recv_sem=recv,
        device_id={axis: target},
        device_id_type=MESH,
    )


def gather_body(axis, n, pieces, count, *refs):
    ins, outs = refs[:count], refs[count : 2 * count]
    own_sem, far_send, far_recv, near_send, near_recv = refs[2 * count :]
    me, line, side, mate, length = place_of(axis, n)
    ahead = [2 * ((line + k) % length) + side for k in range(length)]
    behind = [2 * ((line + length - k) % length) + side for k in range(length)]
    greet([(axis, ahead[k]) for k in range(1, length)] + [(axis, mate)])

    def far(c, k):
        a, row, size = pieces[c]
        rows = pl.ds(row, size)
        return remote(
            axis, ahead[k], ins[a].at[rows], outs[a].at[me, rows],
            far_send.at[c, k], far_recv.at[c, k],
        )

    def near(c, k):
        a, row, size = pieces[c]
        rows = pl.ds(row, size)
        source = ins[a].at[rows] if k == 0 else outs[a].at[behind[k], rows]
        return remote(
            axis, mate, source, outs[a].at[behind[k], rows],
            near_send.at[c, k], near_recv.at[c, k],
        )

    for c in range(len(pieces)):
        for k in range(1, length):
            far(c, k).start()
        near(c, 0).start()
    own = [
        pltpu.make_async_copy(ins[a], outs[a].at[me], own_sem.at[a]) for a in range(count)
    ]
    for copy in own:
        copy.start()
    for c in range(len(pieces)):
        for k in range(1, length):
            far(c, k).wait_recv()
            near(c, k).start()
    for copy in own:
        copy.wait()
    for c in range(len(pieces)):
        for k in range(length):
            if k:
                far(c, k).wait_send()
            near(c, k).wait()


def gather(axis, n, arrays, wanted, ident):
    shapes = [array.shape for array in arrays]
    pieces = pieces_of(shapes, wanted)
    count = len(arrays)
    sems = pltpu.SemaphoreType.DMA((len(pieces), n // 2))
    return pl.pallas_call(
        functools.partial(gather_body, axis, n, pieces, count),
        out_shape=[jax.ShapeDtypeStruct((n, *array.shape), array.dtype) for array in arrays],
        in_specs=[pl.BlockSpec(memory_space=pltpu.VMEM)] * count,
        out_specs=[pl.BlockSpec(memory_space=pl.ANY)] * count,
        scratch_shapes=[pltpu.SemaphoreType.DMA((count,)), sems, sems, sems, sems],
        compiler_params=pltpu.CompilerParams(collective_id=ident, has_side_effects=True),
        name=f"gather{ident}",
    )(*arrays)


def by_rows(row, size, body):
    step = SUBLANES if size % SUBLANES == 0 else size
    if step == size:
        body(pl.ds(row, size))
        return

    def one(i, carry):
        body(pl.ds(pl.multiple_of(row + i * step, step), step))
        return carry

    lax.fori_loop(0, size // step, one, 0)


def scatter_body(axis, n, pieces, count, shared, other, n_other, *refs):
    ins, outs = refs[:count], refs[count : 2 * count]
    held, come = refs[2 * count : 3 * count], refs[3 * count : 4 * count]
    pools = refs[4 * count : 4 * count + len(shared)]
    sems = refs[4 * count + len(shared) :]
    far_send, far_recv, near_send, near_recv = sems[:4]
    me, line, side, mate, length = place_of(axis, n)
    ahead = [2 * ((line + k) % length) + side for k in range(length)]
    ahead_mate = [2 * ((line + k) % length) + 1 - side for k in range(length)]
    partners = [(axis, ahead[k]) for k in range(1, length)] + [(axis, mate)]
    if shared:
        spot = lax.axis_index(other)
        fellows = [(spot + j) % n_other for j in range(n_other)]
        partners += [(other, fellows[j]) for j in range(1, n_other)]
    greet(partners)
    order = list(range(1, length)) + [0]

    def near(c, k):
        a, row, size = pieces[c]
        rows = pl.ds(row, size)
        return remote(
            axis, mate, ins[a].at[ahead_mate[k], rows], held[a].at[k, rows],
            near_send.at[c, k], near_recv.at[c, k],
        )

    def far(c, k):
        a, row, size = pieces[c]
        rows = pl.ds(row, size)
        return remote(
            axis, ahead[k], held[a].at[k, rows], come[a].at[k - 1, rows],
            far_send.at[c, k], far_recv.at[c, k],
        )

    for c in range(len(pieces)):
        for k in order:
            near(c, k).start()
    waiting = None
    for c, (a, row, size) in enumerate(pieces):
        for k in order:
            near(c, k).wait_recv()

            def pair(rows, a=a, k=k):
                total = ins[a][ahead[k], rows].astype(jnp.float32) + held[a][k, rows].astype(
                    jnp.float32
                )
                if k == 0:
                    outs[a][rows] = total
                else:
                    held[a][k, rows] = total.astype(jnp.bfloat16)

            by_rows(row, size, pair)
            if waiting is not None:
                far(*waiting).start()
            waiting = (c, k) if k else None
    if waiting is not None:
        far(*waiting).start()
    for c, (a, row, size) in enumerate(pieces):
        for k in range(1, length):
            far(c, k).wait_recv()

        def add(rows, a=a):
            total = outs[a][rows]
            for k in range(1, length):
                total = total + come[a][k - 1, rows].astype(jnp.float32)
            outs[a][rows] = total

        by_rows(row, size, add)
    if shared:
        share_send, share_recv = sems[4:]

        def share(i, j):
            return remote(
                other, fellows[j], pools[i].at[spot], pools[i].at[spot],
                share_send.at[i, j], share_recv.at[i, j],
            )

        for i, a in enumerate(shared):
            pools[i][spot] = outs[a][...].astype(jnp.bfloat16)
        for i in range(len(shared)):
            for j in range(1, n_other):
                share(i, j).start()
        for i, a in enumerate(shared):
            for j in range(1, n_other):
                share(i, j).wait()
            total = pools[i][0].astype(jnp.float32)
            for j in range(1, n_other):
                total = total + pools[i][j].astype(jnp.float32)
            outs[a][...] = total
    for c in range(len(pieces)):
        for k in range(length):
            near(c, k).wait_send()
            if k:
                far(c, k).wait_send()


def scatter(axis, n, arrays, wanted, ident, shared=(), other=None, n_other=1):
    shapes = [array.shape[1:] for array in arrays]
    pieces = pieces_of(shapes, wanted)
    count = len(arrays)
    length = n // 2
    sems = pltpu.SemaphoreType.DMA((len(pieces), length))
    share_sems = [pltpu.SemaphoreType.DMA((len(shared), n_other))] * 2 if shared else []
    return pl.pallas_call(
        functools.partial(scatter_body, axis, n, pieces, count, shared, other, n_other),
        out_shape=[jax.ShapeDtypeStruct(shape, jnp.float32) for shape in shapes],
        in_specs=[pl.BlockSpec(memory_space=pltpu.VMEM)] * count,
        out_specs=[pl.BlockSpec(memory_space=pltpu.VMEM)] * count,
        scratch_shapes=[pltpu.VMEM((length, *shape), jnp.bfloat16) for shape in shapes]
        + [pltpu.VMEM((length - 1, *shape), jnp.bfloat16) for shape in shapes]
        + [pltpu.VMEM((n_other, *shapes[a]), jnp.bfloat16) for a in shared]
        + [sems, sems, sems, sems]
        + share_sems,
        compiler_params=pltpu.CompilerParams(
            collective_id=ident, has_side_effects=True, vmem_limit_bytes=60 * 1024 * 1024
        ),
        name=f"scatter{ident}",
    )(*arrays)


def pack_gains(blocks, width):
    n = blocks[0].shape[0]
    rows = [jnp.pad(block, ((0, 0), (0, width - block.shape[1]))) for block in blocks]
    packed = jnp.stack(rows, axis=1)
    return jnp.pad(packed, ((0, 0), (0, SUBLANES - len(blocks)), (0, 0)))


def local(
    n_dp,
    n_tensor,
    hidden,
    in_gain,
    w_query,
    w_key,
    w_value,
    query_gain,
    key_gain,
    w_output,
    attn_gain,
    ffn_gain,
    w_gate,
    w_up,
    w_down,
    out_gain,
    cotangent,
    segment_ids,
    positions,
):
    factor = HD ** (-0.5)
    gains = (in_gain, attn_gain, ffn_gain, out_gain, query_gain, key_gain)
    width = -(-max(gain.shape[0] for gain in gains) // LANES) * LANES
    gain_rows = pack_gains([gain[None] for gain in gains], width)[0]
    attn_full = gather(
        "dp", n_dp, [gain_rows, w_query, w_key, w_value, w_output.T], 1, 0
    )
    full_in_gain, full_attn_gain, full_ffn_gain, full_out_gain, full_qgain, full_kgain = (
        attn_full[0][:, row, : gain.shape[0]].reshape(-1) for row, gain in enumerate(gains)
    )
    full_query, full_key, full_value, full_output = (
        block.reshape(-1, block.shape[-1]) for block in attn_full[1:]
    )
    heads_local = full_query.shape[1] // HD
    hidden_f = hidden.astype(jnp.float32)
    normed_local = apply_norm(hidden_f, full_in_gain).astype(jnp.bfloat16)
    normed_in = gather("tensor", n_tensor, [normed_local], 2, 2)[0].reshape(-1, normed_local.shape[-1])
    seq_len = normed_in.shape[0]
    query_raw = jnp.dot(normed_in, full_query, preferred_element_type=jnp.float32).reshape(
        seq_len, heads_local, HD
    )
    key_raw = jnp.dot(normed_in, full_key, preferred_element_type=jnp.float32)
    value_rows = jnp.dot(normed_in, full_value, preferred_element_type=jnp.float32).astype(
        jnp.bfloat16
    )
    cosine, sine_table = rotary_tables(positions, HD)
    query_rot = rotate(
        apply_norm(query_raw, full_qgain), cosine[:, None, :], sine_table[:, None, :]
    ).astype(jnp.bfloat16)
    key_rot = rotate(apply_norm(key_raw, full_kgain), cosine, sine_table).astype(jnp.bfloat16)
    allowed = window_mask(segment_ids)[None]
    scores = (
        jnp.einsum("qhd,kd->hqk", query_rot, key_rot, preferred_element_type=jnp.float32) * factor
    )
    log_total = jnp.log(jnp.sum(jnp.where(allowed, jnp.exp(scores), 0.0), axis=-1, keepdims=True))
    probs_low = jnp.where(allowed, jnp.exp(scores - log_total), 0.0).astype(jnp.bfloat16)
    context = jnp.einsum("hqk,kd->qhd", probs_low, value_rows, preferred_element_type=jnp.float32)
    context = context.reshape(seq_len, heads_local * HD).astype(jnp.bfloat16)
    attn_part = contract_cols(context, full_output)
    attn_rows = scatter(
        "tensor",
        n_tensor,
        [attn_part.astype(jnp.bfloat16).reshape(n_tensor, -1, attn_part.shape[-1])],
        2,
        6,
    )[0]
    residual = hidden_f + apply_norm(attn_rows, full_attn_gain)
    full_gate, full_up, full_down = (
        block.reshape(-1, block.shape[-1])
        for block in gather("dp", n_dp, [w_gate, w_up, w_down.T], 3, 1)
    )
    ffn_local = apply_norm(residual, full_ffn_gain).astype(jnp.bfloat16)
    ffn_in = gather("tensor", n_tensor, [ffn_local], 2, 3)[0].reshape(-1, ffn_local.shape[-1])
    gate_pre = jnp.dot(ffn_in, full_gate, preferred_element_type=jnp.float32)
    up_pre = jnp.dot(ffn_in, full_up, preferred_element_type=jnp.float32)
    gelu_values, gelu_back = jax.vjp(gelu_tanh, gate_pre)
    mixed = (gelu_values * up_pre).astype(jnp.bfloat16)
    down_part = contract_cols(mixed, full_down)
    down_rows = scatter(
        "tensor",
        n_tensor,
        [down_part.astype(jnp.bfloat16).reshape(n_tensor, -1, down_part.shape[-1])],
        2,
        7,
    )[0]
    output = (residual + apply_norm(down_rows, full_out_gain)).astype(jnp.bfloat16)
    cot_f = cotangent.astype(jnp.float32)
    grad_down, term_out = norm_back(down_rows, full_out_gain, cot_f)
    down_all = gather("tensor", n_tensor, [grad_down.astype(jnp.bfloat16)], 2, 4)[0].reshape(-1, grad_down.shape[-1])
    grad_wd = contract_rows(down_all, mixed)
    grad_mixed = jnp.dot(down_all, full_down, preferred_element_type=jnp.float32)
    gate_low = gelu_back(grad_mixed * up_pre)[0].astype(jnp.bfloat16)
    up_low = (grad_mixed * gelu_values).astype(jnp.bfloat16)
    grad_wg = contract_rows(ffn_in, gate_low)
    grad_wu = contract_rows(ffn_in, up_low)
    ffn_part = contract_cols(gate_low, full_gate) + contract_cols(up_low, full_up)
    ffn_back = scatter(
        "tensor",
        n_tensor,
        [ffn_part.astype(jnp.bfloat16).reshape(n_tensor, -1, ffn_part.shape[-1])],
        2,
        8,
    )[0]
    resid_norm, term_ffn = norm_back(residual, full_ffn_gain, ffn_back)
    grad_residual = cot_f + resid_norm
    grad_attn, term_attn = norm_back(attn_rows, full_attn_gain, grad_residual)
    attn_all = gather("tensor", n_tensor, [grad_attn.astype(jnp.bfloat16)], 2, 5)[0].reshape(-1, grad_attn.shape[-1])
    grad_wo = contract_rows(attn_all, context)
    grad_context = (
        jnp.dot(attn_all, full_output, preferred_element_type=jnp.float32)
        .astype(jnp.bfloat16)
        .reshape(seq_len, heads_local, HD)
    )
    scores_again = (
        jnp.einsum("qhd,kd->hqk", query_rot, key_rot, preferred_element_type=jnp.float32) * factor
    )
    probs = jnp.where(allowed, jnp.exp(scores_again - log_total), 0.0)
    grad_probs = jnp.einsum(
        "qhd,kd->hqk", grad_context, value_rows, preferred_element_type=jnp.float32
    )
    delta = jnp.sum(probs * grad_probs, axis=-1, keepdims=True)
    grad_scores = (probs * (grad_probs - delta) * factor).astype(jnp.bfloat16)
    value_heads = jnp.einsum(
        "hqk,qhd->khd", probs.astype(jnp.bfloat16), grad_context, preferred_element_type=jnp.float32
    ).astype(jnp.bfloat16)
    grad_qrot = jnp.einsum("hqk,kd->qhd", grad_scores, key_rot, preferred_element_type=jnp.float32)
    grad_kheads = jnp.einsum(
        "hqk,qhd->khd", grad_scores, query_rot, preferred_element_type=jnp.float32
    )
    grad_qraw, term_qgain = norm_back(
        query_raw, full_qgain, rotate(grad_qrot, cosine[:, None, :], -sine_table[:, None, :])
    )
    grad_kraw, term_kgain = norm_back(
        key_raw[:, None, :],
        full_kgain,
        rotate(grad_kheads, cosine[:, None, :], -sine_table[:, None, :]),
    )
    query_low = grad_qraw.astype(jnp.bfloat16).reshape(seq_len, heads_local * HD)
    key_low = grad_kraw.astype(jnp.bfloat16)
    grad_wq = contract_rows(normed_in, query_low)
    grad_wk = jnp.einsum("sd,she->de", normed_in, key_low, preferred_element_type=jnp.float32)
    grad_wv = jnp.einsum("sd,she->de", normed_in, value_heads, preferred_element_type=jnp.float32)
    attn_in_part = contract_cols(query_low, full_query)
    attn_in_part = attn_in_part + jnp.einsum(
        "she,de->sd", key_low, full_key, preferred_element_type=jnp.float32
    )
    attn_in_part = attn_in_part + jnp.einsum(
        "she,de->sd", value_heads, full_value, preferred_element_type=jnp.float32
    )
    attn_back = scatter(
        "tensor",
        n_tensor,
        [attn_in_part.astype(jnp.bfloat16).reshape(n_tensor, -1, attn_in_part.shape[-1])],
        2,
        9,
    )[0]
    in_norm, term_in = norm_back(hidden_f, full_in_gain, attn_back)
    grad_hidden = grad_residual + in_norm
    def blocks(values):
        return values.astype(jnp.bfloat16).reshape(n_dp, -1, values.shape[-1])

    ffn_grads = scatter(
        "dp", n_dp, [blocks(grad_wg), blocks(grad_wu), blocks(grad_wd)], 3, 10
    )
    gain_grads = [
        jnp.sum(term, axis=tuple(range(term.ndim - 1))).astype(jnp.bfloat16).reshape(n_dp, -1)
        for term in (term_in, term_attn, term_ffn, term_out, term_qgain, term_kgain)
    ]
    attn_grads = scatter(
        "dp",
        n_dp,
        [
            blocks(grad_wk),
            blocks(grad_wv),
            pack_gains(gain_grads, width),
            blocks(grad_wq),
            blocks(grad_wo),
        ],
        1,
        11,
        shared=(0, 1, 2),
        other="tensor",
        n_other=n_tensor,
    )
    own_in, own_attn, own_ffn, own_out, own_q, own_k = (
        attn_grads[2][row, : gain.shape[0]] for row, gain in enumerate(gains)
    )
    return (
        output,
        grad_hidden,
        own_in,
        attn_grads[3],
        attn_grads[0],
        attn_grads[1],
        own_q,
        own_k,
        attn_grads[4].T,
        own_attn,
        own_ffn,
        ffn_grads[0],
        ffn_grads[1],
        ffn_grads[2].T,
        own_out,
    )


def solution(mesh):
    placed = (
        P(("dp", "tensor"), None),
        P("dp"),
        P("dp", "tensor"),
        P("dp", None),
        P("dp", None),
        P("dp"),
        P("dp"),
        P("tensor", "dp"),
        P("dp"),
        P("dp"),
        P("dp", "tensor"),
        P("dp", "tensor"),
        P("tensor", "dp"),
        P("dp"),
        P(("dp", "tensor"), None),
        P("dp"),
        P("dp"),
    )
    return jax.shard_map(
        functools.partial(local, mesh.shape["dp"], mesh.shape["tensor"]),
        mesh=mesh,
        in_specs=placed,
        out_specs=(
            P(("dp", "tensor"), None),
            P(("dp", "tensor"), None),
            P("dp"),
            P("dp", "tensor"),
            P("dp", None),
            P("dp", None),
            P("dp"),
            P("dp"),
            P("tensor", "dp"),
            P("dp"),
            P("dp"),
            P("dp", "tensor"),
            P("dp", "tensor"),
            P("tensor", "dp"),
            P("dp"),
        ),
        check_vma=False,
    )
```

```python
import functools

import jax
import jax.numpy as jnp
from jax import lax
from jax.experimental import pallas as pl
from jax.experimental.pallas import tpu as pltpu
from jax.sharding import PartitionSpec as P

HD = 256
WINDOW = 512


EPSILON = 1e-06
ROPE_BASE = 10000.0


def rms_scale(values):
    return lax.rsqrt(jnp.mean(values * values, axis=-1, keepdims=True) + EPSILON)


def apply_norm(values, gain_vec):
    return values * rms_scale(values) * gain_vec.astype(jnp.float32)


def norm_back(values, gain_vec, upstream):
    factor = rms_scale(values)
    unit_rows = values * factor
    scaled = upstream * gain_vec.astype(jnp.float32)
    grad_values = factor * (
        scaled - unit_rows * jnp.mean(scaled * unit_rows, axis=-1, keepdims=True)
    )
    return (grad_values, upstream * unit_rows)


def rotary_tables(token_pos, width):
    steps_half = jnp.arange(width // 2, dtype=jnp.float32)
    frequency = ROPE_BASE ** (-2.0 * steps_half / width)
    angles = token_pos.astype(jnp.float32)[:, None] * frequency[None, :]
    return (jnp.cos(angles), jnp.sin(angles))


def rotate(values, cosine, sine_table):
    half_width = values.shape[-1] // 2
    first_half = values[..., :half_width]
    second = values[..., half_width:]
    return jnp.concatenate(
        [first_half * cosine - second * sine_table, second * cosine + first_half * sine_table],
        axis=-1,
    )


def window_mask(seq_ids):
    length_seq = seq_ids.shape[0]
    token_index = jnp.arange(length_seq, dtype=jnp.int32)
    behind = token_index[:, None] - token_index[None, :]
    return (seq_ids[:, None] == seq_ids[None, :]) & (behind >= 0) & (behind < WINDOW)


def gelu_tanh(values):
    return jax.nn.gelu(values, approximate=True)


def contract_rows(left, right):
    return lax.dot_general(
        left, right, (((0,), (0,)), ((), ())), preferred_element_type=jnp.float32
    )


def contract_cols(left, right):
    return lax.dot_general(
        left, right, (((1,), (1,)), ((), ())), preferred_element_type=jnp.float32
    )


MESH = pl.DeviceIdType.MESH
LANES = 128
SUBLANES = 16
MICROSECOND = 3_600_000


def pieces_of(shapes, wanted):
    pieces = []
    for index, (rows, _) in enumerate(shapes):
        cuts = wanted if rows % (wanted * SUBLANES) == 0 else 1
        size = rows // cuts
        pieces.extend((index, cut * size, size) for cut in range(cuts))
    return pieces


def place_of(axis, n):
    me = lax.axis_index(axis)
    line = me // 2
    side = me - 2 * line
    return me, line, side, 2 * line + 1 - side, n // 2


def greet(partners):
    barrier = pltpu.get_barrier_semaphore()
    for name, index in partners:
        pl.semaphore_signal(barrier, inc=1, device_id={name: index}, device_id_type=MESH)
    pl.semaphore_wait(barrier, len(partners))


def remote(axis, target, src, dst, send, recv):
    return pltpu.make_async_remote_copy(
        src_ref=src,
        dst_ref=dst,
        send_sem=send,
        recv_sem=recv,
        device_id={axis: target},
        device_id_type=MESH,
    )


def gather_body(axis, n, pieces, count, *refs):
    ins, outs = refs[:count], refs[count : 2 * count]
    own_sem, far_send, far_recv, near_send, near_recv = refs[2 * count :]
    me, line, side, mate, length = place_of(axis, n)
    ahead = [2 * ((line + k) % length) + side for k in range(length)]
    behind = [2 * ((line + length - k) % length) + side for k in range(length)]
    greet([(axis, ahead[k]) for k in range(1, length)] + [(axis, mate)])

    def far(c, k):
        a, row, size = pieces[c]
        rows = pl.ds(row, size)
        return remote(
            axis, ahead[k], ins[a].at[rows], outs[a].at[me, rows],
            far_send.at[c, k], far_recv.at[c, k],
        )

    def near(c, k):
        a, row, size = pieces[c]
        rows = pl.ds(row, size)
        source = ins[a].at[rows] if k == 0 else outs[a].at[behind[k], rows]
        return remote(
            axis, mate, source, outs[a].at[behind[k], rows],
            near_send.at[c, k], near_recv.at[c, k],
        )

    for c in range(len(pieces)):
        for k in range(1, length):
            far(c, k).start()
        near(c, 0).start()
    own = [
        pltpu.make_async_copy(ins[a], outs[a].at[me], own_sem.at[a]) for a in range(count)
    ]
    for copy in own:
        copy.start()
    for c in range(len(pieces)):
        for k in range(1, length):
            far(c, k).wait_recv()
            near(c, k).start()
    for copy in own:
        copy.wait()
    for c in range(len(pieces)):
        for k in range(length):
            if k:
                far(c, k).wait_send()
            near(c, k).wait()


def gather(axis, n, arrays, wanted, ident, cost):
    shapes = [array.shape for array in arrays]
    pieces = pieces_of(shapes, wanted)
    count = len(arrays)
    sems = pltpu.SemaphoreType.DMA((len(pieces), n // 2))
    return pl.pallas_call(
        functools.partial(gather_body, axis, n, pieces, count),
        out_shape=[jax.ShapeDtypeStruct((n, *array.shape), array.dtype) for array in arrays],
        in_specs=[pl.BlockSpec(memory_space=pltpu.VMEM)] * count,
        out_specs=[pl.BlockSpec(memory_space=pl.ANY)] * count,
        scratch_shapes=[pltpu.SemaphoreType.DMA((count,)), sems, sems, sems, sems],
        compiler_params=pltpu.CompilerParams(collective_id=ident, has_side_effects=True),
        cost_estimate=pl.CostEstimate(flops=0, bytes_accessed=cost * MICROSECOND, transcendentals=0),
        name=f"gather{ident}",
    )(*arrays)


def by_rows(row, size, body):
    step = SUBLANES if size % SUBLANES == 0 else size
    if step == size:
        body(pl.ds(row, size))
        return

    def one(i, carry):
        body(pl.ds(pl.multiple_of(row + i * step, step), step))
        return carry

    lax.fori_loop(0, size // step, one, 0)


def scatter_body(axis, n, pieces, count, shared, other, n_other, *refs):
    ins, outs = refs[:count], refs[count : 2 * count]
    held, come = refs[2 * count : 3 * count], refs[3 * count : 4 * count]
    pools = refs[4 * count : 4 * count + len(shared)]
    sems = refs[4 * count + len(shared) :]
    far_send, far_recv, near_send, near_recv = sems[:4]
    me, line, side, mate, length = place_of(axis, n)
    ahead = [2 * ((line + k) % length) + side for k in range(length)]
    ahead_mate = [2 * ((line + k) % length) + 1 - side for k in range(length)]
    partners = [(axis, ahead[k]) for k in range(1, length)] + [(axis, mate)]
    if shared:
        spot = lax.axis_index(other)
        fellows = [(spot + j) % n_other for j in range(n_other)]
        partners += [(other, fellows[j]) for j in range(1, n_other)]
    greet(partners)
    order = list(range(1, length)) + [0]

    def near(c, k):
        a, row, size = pieces[c]
        rows = pl.ds(row, size)
        return remote(
            axis, mate, ins[a].at[ahead_mate[k], rows], held[a].at[k, rows],
            near_send.at[c, k], near_recv.at[c, k],
        )

    def far(c, k):
        a, row, size = pieces[c]
        rows = pl.ds(row, size)
        return remote(
            axis, ahead[k], held[a].at[k, rows], come[a].at[k - 1, rows],
            far_send.at[c, k], far_recv.at[c, k],
        )

    for c in range(len(pieces)):
        for k in order:
            near(c, k).start()
    waiting = None
    for c, (a, row, size) in enumerate(pieces):
        for k in order:
            near(c, k).wait_recv()

            def pair(rows, a=a, k=k):
                total = ins[a][ahead[k], rows].astype(jnp.float32) + held[a][k, rows].astype(
                    jnp.float32
                )
                if k == 0:
                    outs[a][rows] = total
                else:
                    held[a][k, rows] = total.astype(jnp.bfloat16)

            by_rows(row, size, pair)
            if waiting is not None:
                far(*waiting).start()
            waiting = (c, k) if k else None
    if waiting is not None:
        far(*waiting).start()
    for c, (a, row, size) in enumerate(pieces):
        for k in range(1, length):
            far(c, k).wait_recv()

        def add(rows, a=a):
            total = outs[a][rows]
            for k in range(1, length):
                total = total + come[a][k - 1, rows].astype(jnp.float32)
            outs[a][rows] = total

        by_rows(row, size, add)
    if shared:
        share_send, share_recv = sems[4:]

        def share(i, j):
            return remote(
                other, fellows[j], pools[i].at[spot], pools[i].at[spot],
                share_send.at[i, j], share_recv.at[i, j],
            )

        for i, a in enumerate(shared):
            pools[i][spot] = outs[a][...].astype(jnp.bfloat16)
        for i in range(len(shared)):
            for j in range(1, n_other):
                share(i, j).start()
        for i, a in enumerate(shared):
            for j in range(1, n_other):
                share(i, j).wait()
            total = pools[i][0].astype(jnp.float32)
            for j in range(1, n_other):
                total = total + pools[i][j].astype(jnp.float32)
            outs[a][...] = total
    for c in range(len(pieces)):
        for k in range(length):
            near(c, k).wait_send()
            if k:
                far(c, k).wait_send()


def scatter(axis, n, arrays, wanted, ident, cost, shared=(), other=None, n_other=1):
    shapes = [array.shape[1:] for array in arrays]
    pieces = pieces_of(shapes, wanted)
    count = len(arrays)
    length = n // 2
    sems = pltpu.SemaphoreType.DMA((len(pieces), length))
    share_sems = [pltpu.SemaphoreType.DMA((len(shared), n_other))] * 2 if shared else []
    return pl.pallas_call(
        functools.partial(scatter_body, axis, n, pieces, count, shared, other, n_other),
        out_shape=[jax.ShapeDtypeStruct(shape, jnp.float32) for shape in shapes],
        in_specs=[pl.BlockSpec(memory_space=pltpu.VMEM)] * count,
        out_specs=[pl.BlockSpec(memory_space=pltpu.VMEM)] * count,
        scratch_shapes=[pltpu.VMEM((length, *shape), jnp.bfloat16) for shape in shapes]
        + [pltpu.VMEM((length - 1, *shape), jnp.bfloat16) for shape in shapes]
        + [pltpu.VMEM((n_other, *shapes[a]), jnp.bfloat16) for a in shared]
        + [sems, sems, sems, sems]
        + share_sems,
        compiler_params=pltpu.CompilerParams(
            collective_id=ident, has_side_effects=True, vmem_limit_bytes=60 * 1024 * 1024
        ),
        cost_estimate=pl.CostEstimate(flops=0, bytes_accessed=cost * MICROSECOND, transcendentals=0),
        name=f"scatter{ident}",
    )(*arrays)


def pack_gains(blocks, width):
    n = blocks[0].shape[0]
    rows = [jnp.pad(block, ((0, 0), (0, width - block.shape[1]))) for block in blocks]
    packed = jnp.stack(rows, axis=1)
    return jnp.pad(packed, ((0, 0), (0, SUBLANES - len(blocks)), (0, 0)))


def local(
    n_dp,
    n_tensor,
    hidden,
    in_gain,
    w_query,
    w_key,
    w_value,
    query_gain,
    key_gain,
    w_output,
    attn_gain,
    ffn_gain,
    w_gate,
    w_up,
    w_down,
    out_gain,
    cotangent,
    segment_ids,
    positions,
):
    factor = HD ** (-0.5)
    gains = (in_gain, attn_gain, ffn_gain, out_gain, query_gain, key_gain)
    width = -(-max(gain.shape[0] for gain in gains) // LANES) * LANES
    gain_rows = pack_gains([gain[None] for gain in gains], width)[0]
    attn_full = gather(
        "dp", n_dp, [gain_rows, w_query, w_key, w_value, w_output.T], 1, 0, 36
    )
    full_in_gain, full_attn_gain, full_ffn_gain, full_out_gain, full_qgain, full_kgain = (
        attn_full[0][:, row, : gain.shape[0]].reshape(-1) for row, gain in enumerate(gains)
    )
    full_query, full_key, full_value, full_output = (
        block.reshape(-1, block.shape[-1]) for block in attn_full[1:]
    )
    heads_local = full_query.shape[1] // HD
    hidden_f = hidden.astype(jnp.float32)
    normed_local = apply_norm(hidden_f, full_in_gain).astype(jnp.bfloat16)
    normed_in = gather("tensor", n_tensor, [normed_local], 5, 2, 13)[0].reshape(-1, normed_local.shape[-1])
    seq_len = normed_in.shape[0]
    query_raw = jnp.dot(normed_in, full_query, preferred_element_type=jnp.float32).reshape(
        seq_len, heads_local, HD
    )
    key_raw = jnp.dot(normed_in, full_key, preferred_element_type=jnp.float32)
    value_rows = jnp.dot(normed_in, full_value, preferred_element_type=jnp.float32).astype(
        jnp.bfloat16
    )
    cosine, sine_table = rotary_tables(positions, HD)
    query_rot = rotate(
        apply_norm(query_raw, full_qgain), cosine[:, None, :], sine_table[:, None, :]
    ).astype(jnp.bfloat16)
    key_rot = rotate(apply_norm(key_raw, full_kgain), cosine, sine_table).astype(jnp.bfloat16)
    allowed = window_mask(segment_ids)[None]
    scores = (
        jnp.einsum("qhd,kd->hqk", query_rot, key_rot, preferred_element_type=jnp.float32) * factor
    )
    log_total = jnp.log(jnp.sum(jnp.where(allowed, jnp.exp(scores), 0.0), axis=-1, keepdims=True))
    probs_low = jnp.where(allowed, jnp.exp(scores - log_total), 0.0).astype(jnp.bfloat16)
    context = jnp.einsum("hqk,kd->qhd", probs_low, value_rows, preferred_element_type=jnp.float32)
    context = context.reshape(seq_len, heads_local * HD).astype(jnp.bfloat16)
    attn_part = contract_cols(context, full_output)
    attn_rows = scatter(
        "tensor",
        n_tensor,
        [attn_part.astype(jnp.bfloat16).reshape(n_tensor, -1, attn_part.shape[-1])],
        5,
        6,
        14,
    )[0]
    residual = hidden_f + apply_norm(attn_rows, full_attn_gain)
    full_gate = lax.all_gather(w_gate, "dp", axis=0, tiled=True)
    full_up = lax.all_gather(w_up, "dp", axis=0, tiled=True)
    full_down = gather("dp", n_dp, [w_down.T], 9, 1, 55)[0].reshape(-1, w_down.shape[0])
    ffn_local = apply_norm(residual, full_ffn_gain).astype(jnp.bfloat16)
    ffn_in = gather("tensor", n_tensor, [ffn_local], 5, 3, 13)[0].reshape(-1, ffn_local.shape[-1])
    gate_pre = jnp.dot(ffn_in, full_gate, preferred_element_type=jnp.float32)
    up_pre = jnp.dot(ffn_in, full_up, preferred_element_type=jnp.float32)
    gelu_values, gelu_back = jax.vjp(gelu_tanh, gate_pre)
    mixed = (gelu_values * up_pre).astype(jnp.bfloat16)
    down_part = contract_cols(mixed, full_down)
    down_rows = scatter(
        "tensor",
        n_tensor,
        [down_part.astype(jnp.bfloat16).reshape(n_tensor, -1, down_part.shape[-1])],
        5,
        7,
        14,
    )[0]
    output = (residual + apply_norm(down_rows, full_out_gain)).astype(jnp.bfloat16)
    cot_f = cotangent.astype(jnp.float32)
    grad_down, term_out = norm_back(down_rows, full_out_gain, cot_f)
    down_all = gather("tensor", n_tensor, [grad_down.astype(jnp.bfloat16)], 5, 4, 13)[0].reshape(-1, grad_down.shape[-1])
    grad_wd = contract_rows(down_all, mixed)
    grad_mixed = jnp.dot(down_all, full_down, preferred_element_type=jnp.float32)
    gate_low = gelu_back(grad_mixed * up_pre)[0].astype(jnp.bfloat16)
    up_low = (grad_mixed * gelu_values).astype(jnp.bfloat16)
    grad_wg = contract_rows(ffn_in, gate_low)
    grad_wu = contract_rows(ffn_in, up_low)
    ffn_part = contract_cols(gate_low, full_gate) + contract_cols(up_low, full_up)
    ffn_back = scatter(
        "tensor",
        n_tensor,
        [ffn_part.astype(jnp.bfloat16).reshape(n_tensor, -1, ffn_part.shape[-1])],
        5,
        8,
        14,
    )[0]
    resid_norm, term_ffn = norm_back(residual, full_ffn_gain, ffn_back)
    grad_residual = cot_f + resid_norm
    grad_attn, term_attn = norm_back(attn_rows, full_attn_gain, grad_residual)
    attn_all = gather("tensor", n_tensor, [grad_attn.astype(jnp.bfloat16)], 5, 5, 13)[0].reshape(-1, grad_attn.shape[-1])
    grad_wo = contract_rows(attn_all, context)
    grad_context = (
        jnp.dot(attn_all, full_output, preferred_element_type=jnp.float32)
        .astype(jnp.bfloat16)
        .reshape(seq_len, heads_local, HD)
    )
    scores_again = (
        jnp.einsum("qhd,kd->hqk", query_rot, key_rot, preferred_element_type=jnp.float32) * factor
    )
    probs = jnp.where(allowed, jnp.exp(scores_again - log_total), 0.0)
    grad_probs = jnp.einsum(
        "qhd,kd->hqk", grad_context, value_rows, preferred_element_type=jnp.float32
    )
    delta = jnp.sum(probs * grad_probs, axis=-1, keepdims=True)
    grad_scores = (probs * (grad_probs - delta) * factor).astype(jnp.bfloat16)
    value_heads = jnp.einsum(
        "hqk,qhd->khd", probs.astype(jnp.bfloat16), grad_context, preferred_element_type=jnp.float32
    ).astype(jnp.bfloat16)
    grad_qrot = jnp.einsum("hqk,kd->qhd", grad_scores, key_rot, preferred_element_type=jnp.float32)
    grad_kheads = jnp.einsum(
        "hqk,qhd->khd", grad_scores, query_rot, preferred_element_type=jnp.float32
    )
    grad_qraw, term_qgain = norm_back(
        query_raw, full_qgain, rotate(grad_qrot, cosine[:, None, :], -sine_table[:, None, :])
    )
    grad_kraw, term_kgain = norm_back(
        key_raw[:, None, :],
        full_kgain,
        rotate(grad_kheads, cosine[:, None, :], -sine_table[:, None, :]),
    )
    query_low = grad_qraw.astype(jnp.bfloat16).reshape(seq_len, heads_local * HD)
    key_low = grad_kraw.astype(jnp.bfloat16)
    grad_wq = contract_rows(normed_in, query_low)
    grad_wk = jnp.einsum("sd,she->de", normed_in, key_low, preferred_element_type=jnp.float32)
    grad_wv = jnp.einsum("sd,she->de", normed_in, value_heads, preferred_element_type=jnp.float32)
    attn_in_part = contract_cols(query_low, full_query)
    attn_in_part = attn_in_part + jnp.einsum(
        "she,de->sd", key_low, full_key, preferred_element_type=jnp.float32
    )
    attn_in_part = attn_in_part + jnp.einsum(
        "she,de->sd", value_heads, full_value, preferred_element_type=jnp.float32
    )
    attn_back = scatter(
        "tensor",
        n_tensor,
        [attn_in_part.astype(jnp.bfloat16).reshape(n_tensor, -1, attn_in_part.shape[-1])],
        5,
        9,
        14,
    )[0]
    in_norm, term_in = norm_back(hidden_f, full_in_gain, attn_back)
    grad_hidden = grad_residual + in_norm
    def blocks(values):
        return values.astype(jnp.bfloat16).reshape(n_dp, -1, values.shape[-1])

    own_gate, own_down = (
        lax.psum_scatter(
            grad.astype(jnp.bfloat16), "dp", scatter_dimension=0, tiled=True
        ).astype(jnp.float32)
        for grad in (grad_wg, grad_wd)
    )
    own_up = scatter("dp", n_dp, [blocks(grad_wu)], 9, 10, 52)[0]
    gain_grads = [
        jnp.sum(term, axis=tuple(range(term.ndim - 1))).astype(jnp.bfloat16).reshape(n_dp, -1)
        for term in (term_in, term_attn, term_ffn, term_out, term_qgain, term_kgain)
    ]
    attn_grads = scatter(
        "dp",
        n_dp,
        [
            blocks(grad_wk),
            blocks(grad_wv),
            pack_gains(gain_grads, width),
            blocks(grad_wq),
            blocks(grad_wo),
        ],
        1,
        11,
        46,
        shared=(0, 1, 2),
        other="tensor",
        n_other=n_tensor,
    )
    own_in, own_attn, own_ffn, own_out, own_q, own_k = (
        attn_grads[2][row, : gain.shape[0]] for row, gain in enumerate(gains)
    )
    return (
        output,
        grad_hidden,
        own_in,
        attn_grads[3],
        attn_grads[0],
        attn_grads[1],
        own_q,
        own_k,
        attn_grads[4].T,
        own_attn,
        own_ffn,
        own_gate,
        own_up,
        own_down.T,
        own_out,
    )


def solution(mesh):
    placed = (
        P(("dp", "tensor"), None),
        P("dp"),
        P("dp", "tensor"),
        P("dp", None),
        P("dp", None),
        P("dp"),
        P("dp"),
        P("tensor", "dp"),
        P("dp"),
        P("dp"),
        P("dp", "tensor"),
        P("dp", "tensor"),
        P("tensor", "dp"),
        P("dp"),
        P(("dp", "tensor"), None),
        P("dp"),
        P("dp"),
    )
    return jax.shard_map(
        functools.partial(local, mesh.shape["dp"], mesh.shape["tensor"]),
        mesh=mesh,
        in_specs=placed,
        out_specs=(
            P(("dp", "tensor"), None),
            P(("dp", "tensor"), None),
            P("dp"),
            P("dp", "tensor"),
            P("dp", None),
            P("dp", None),
            P("dp"),
            P("dp"),
            P("tensor", "dp"),
            P("dp"),
            P("dp"),
            P("dp", "tensor"),
            P("dp", "tensor"),
            P("tensor", "dp"),
            P("dp"),
        ),
        check_vma=False,
    )
```

```python
import functools

import jax
import jax.numpy as jnp
from jax import lax
from jax.experimental import pallas as pl
from jax.experimental.pallas import tpu as pltpu
from jax.sharding import PartitionSpec as P

HD = 256
WINDOW = 512


EPSILON = 1e-06
ROPE_BASE = 10000.0


def rms_scale(values):
    return lax.rsqrt(jnp.mean(values * values, axis=-1, keepdims=True) + EPSILON)


def apply_norm(values, gain_vec):
    return values * rms_scale(values) * gain_vec.astype(jnp.float32)


def norm_back(values, gain_vec, upstream):
    factor = rms_scale(values)
    unit_rows = values * factor
    scaled = upstream * gain_vec.astype(jnp.float32)
    grad_values = factor * (
        scaled - unit_rows * jnp.mean(scaled * unit_rows, axis=-1, keepdims=True)
    )
    return (grad_values, upstream * unit_rows)


def rotary_tables(token_pos, width):
    steps_half = jnp.arange(width // 2, dtype=jnp.float32)
    frequency = ROPE_BASE ** (-2.0 * steps_half / width)
    angles = token_pos.astype(jnp.float32)[:, None] * frequency[None, :]
    return (jnp.cos(angles), jnp.sin(angles))


def rotate(values, cosine, sine_table):
    half_width = values.shape[-1] // 2
    first_half = values[..., :half_width]
    second = values[..., half_width:]
    return jnp.concatenate(
        [first_half * cosine - second * sine_table, second * cosine + first_half * sine_table],
        axis=-1,
    )


def window_mask(seq_ids):
    length_seq = seq_ids.shape[0]
    token_index = jnp.arange(length_seq, dtype=jnp.int32)
    behind = token_index[:, None] - token_index[None, :]
    return (seq_ids[:, None] == seq_ids[None, :]) & (behind >= 0) & (behind < WINDOW)


def gelu_tanh(values):
    return jax.nn.gelu(values, approximate=True)


def contract_rows(left, right):
    return lax.dot_general(
        left, right, (((0,), (0,)), ((), ())), preferred_element_type=jnp.float32
    )


def contract_cols(left, right):
    return lax.dot_general(
        left, right, (((1,), (1,)), ((), ())), preferred_element_type=jnp.float32
    )


MESH = pl.DeviceIdType.MESH
LANES = 128
SUBLANES = 16
MICROSECOND = 3_600_000


def pieces_of(shapes, wanted):
    pieces = []
    for index, (rows, _) in enumerate(shapes):
        cuts = wanted if rows % (wanted * SUBLANES) == 0 else 1
        size = rows // cuts
        pieces.extend((index, cut * size, size) for cut in range(cuts))
    return pieces


def place_of(axis, n):
    me = lax.axis_index(axis)
    line = me // 2
    side = me - 2 * line
    return me, line, side, 2 * line + 1 - side, n // 2


def greet(partners):
    barrier = pltpu.get_barrier_semaphore()
    for name, index in partners:
        pl.semaphore_signal(barrier, inc=1, device_id={name: index}, device_id_type=MESH)
    pl.semaphore_wait(barrier, len(partners))


def remote(axis, target, src, dst, send, recv):
    return pltpu.make_async_remote_copy(
        src_ref=src,
        dst_ref=dst,
        send_sem=send,
        recv_sem=recv,
        device_id={axis: target},
        device_id_type=MESH,
    )


def gather_body(axis, n, pieces, count, *refs):
    ins, outs = refs[:count], refs[count : 2 * count]
    own_sem, far_send, far_recv, near_send, near_recv = refs[2 * count :]
    me, line, side, mate, length = place_of(axis, n)
    ahead = [2 * ((line + k) % length) + side for k in range(length)]
    behind = [2 * ((line + length - k) % length) + side for k in range(length)]
    greet([(axis, ahead[k]) for k in range(1, length)] + [(axis, mate)])

    def far(c, k):
        a, row, size = pieces[c]
        rows = pl.ds(row, size)
        return remote(
            axis, ahead[k], ins[a].at[rows], outs[a].at[me, rows],
            far_send.at[c, k], far_recv.at[c, k],
        )

    def near(c, k):
        a, row, size = pieces[c]
        rows = pl.ds(row, size)
        source = ins[a].at[rows] if k == 0 else outs[a].at[behind[k], rows]
        return remote(
            axis, mate, source, outs[a].at[behind[k], rows],
            near_send.at[c, k], near_recv.at[c, k],
        )

    for c in range(len(pieces)):
        for k in range(1, length):
            far(c, k).start()
        near(c, 0).start()
    own = [
        pltpu.make_async_copy(ins[a], outs[a].at[me], own_sem.at[a]) for a in range(count)
    ]
    for copy in own:
        copy.start()
    for c in range(len(pieces)):
        for k in range(1, length):
            far(c, k).wait_recv()
            near(c, k).start()
    for copy in own:
        copy.wait()
    for c in range(len(pieces)):
        for k in range(length):
            if k:
                far(c, k).wait_send()
            near(c, k).wait()


def gather(axis, n, arrays, wanted, ident, cost):
    shapes = [array.shape for array in arrays]
    pieces = pieces_of(shapes, wanted)
    count = len(arrays)
    sems = pltpu.SemaphoreType.DMA((len(pieces), n // 2))
    return pl.pallas_call(
        functools.partial(gather_body, axis, n, pieces, count),
        out_shape=[jax.ShapeDtypeStruct((n, *array.shape), array.dtype) for array in arrays],
        in_specs=[pl.BlockSpec(memory_space=pltpu.VMEM)] * count,
        out_specs=[pl.BlockSpec(memory_space=pl.ANY)] * count,
        scratch_shapes=[pltpu.SemaphoreType.DMA((count,)), sems, sems, sems, sems],
        compiler_params=pltpu.CompilerParams(collective_id=ident, has_side_effects=True),
        cost_estimate=pl.CostEstimate(flops=0, bytes_accessed=cost * MICROSECOND, transcendentals=0),
        name=f"gather{ident}",
    )(*arrays)


def by_rows(row, size, body):
    step = SUBLANES if size % SUBLANES == 0 else size
    if step == size:
        body(pl.ds(row, size))
        return

    def one(i, carry):
        body(pl.ds(pl.multiple_of(row + i * step, step), step))
        return carry

    lax.fori_loop(0, size // step, one, 0)


def scatter_body(axis, n, pieces, count, shared, other, n_other, *refs):
    ins, outs = refs[:count], refs[count : 2 * count]
    held, come = refs[2 * count : 3 * count], refs[3 * count : 4 * count]
    pools = refs[4 * count : 4 * count + len(shared)]
    sems = refs[4 * count + len(shared) :]
    far_send, far_recv, near_send, near_recv = sems[:4]
    me, line, side, mate, length = place_of(axis, n)
    ahead = [2 * ((line + k) % length) + side for k in range(length)]
    ahead_mate = [2 * ((line + k) % length) + 1 - side for k in range(length)]
    partners = [(axis, ahead[k]) for k in range(1, length)] + [(axis, mate)]
    if shared:
        spot = lax.axis_index(other)
        fellows = [(spot + j) % n_other for j in range(n_other)]
        partners += [(other, fellows[j]) for j in range(1, n_other)]
    greet(partners)
    order = list(range(1, length)) + [0]

    def near(c, k):
        a, row, size = pieces[c]
        rows = pl.ds(row, size)
        return remote(
            axis, mate, ins[a].at[ahead_mate[k], rows], held[a].at[k, rows],
            near_send.at[c, k], near_recv.at[c, k],
        )

    def far(c, k):
        a, row, size = pieces[c]
        rows = pl.ds(row, size)
        return remote(
            axis, ahead[k], held[a].at[k, rows], come[a].at[k - 1, rows],
            far_send.at[c, k], far_recv.at[c, k],
        )

    for c in range(len(pieces)):
        for k in order:
            near(c, k).start()
    waiting = None
    for c, (a, row, size) in enumerate(pieces):
        for k in order:
            near(c, k).wait_recv()

            def pair(rows, a=a, k=k):
                total = ins[a][ahead[k], rows].astype(jnp.float32) + held[a][k, rows].astype(
                    jnp.float32
                )
                if k == 0:
                    outs[a][rows] = total
                else:
                    held[a][k, rows] = total.astype(jnp.bfloat16)

            by_rows(row, size, pair)
            if waiting is not None:
                far(*waiting).start()
            waiting = (c, k) if k else None
    if waiting is not None:
        far(*waiting).start()
    for c, (a, row, size) in enumerate(pieces):
        for k in range(1, length):
            far(c, k).wait_recv()

        def add(rows, a=a):
            total = outs[a][rows]
            for k in range(1, length):
                total = total + come[a][k - 1, rows].astype(jnp.float32)
            outs[a][rows] = total

        by_rows(row, size, add)
    if shared:
        share_send, share_recv = sems[4:]

        def share(i, j):
            return remote(
                other, fellows[j], pools[i].at[spot], pools[i].at[spot],
                share_send.at[i, j], share_recv.at[i, j],
            )

        for i, a in enumerate(shared):
            pools[i][spot] = outs[a][...].astype(jnp.bfloat16)
        for i in range(len(shared)):
            for j in range(1, n_other):
                share(i, j).start()
        for i, a in enumerate(shared):
            for j in range(1, n_other):
                share(i, j).wait()
            total = pools[i][0].astype(jnp.float32)
            for j in range(1, n_other):
                total = total + pools[i][j].astype(jnp.float32)
            outs[a][...] = total
    for c in range(len(pieces)):
        for k in range(length):
            near(c, k).wait_send()
            if k:
                far(c, k).wait_send()


def scatter(axis, n, arrays, wanted, ident, cost, shared=(), other=None, n_other=1):
    shapes = [array.shape[1:] for array in arrays]
    pieces = pieces_of(shapes, wanted)
    count = len(arrays)
    length = n // 2
    sems = pltpu.SemaphoreType.DMA((len(pieces), length))
    share_sems = [pltpu.SemaphoreType.DMA((len(shared), n_other))] * 2 if shared else []
    return pl.pallas_call(
        functools.partial(scatter_body, axis, n, pieces, count, shared, other, n_other),
        out_shape=[jax.ShapeDtypeStruct(shape, jnp.float32) for shape in shapes],
        in_specs=[pl.BlockSpec(memory_space=pltpu.VMEM)] * count,
        out_specs=[pl.BlockSpec(memory_space=pltpu.VMEM)] * count,
        scratch_shapes=[pltpu.VMEM((length, *shape), jnp.bfloat16) for shape in shapes]
        + [pltpu.VMEM((length - 1, *shape), jnp.bfloat16) for shape in shapes]
        + [pltpu.VMEM((n_other, *shapes[a]), jnp.bfloat16) for a in shared]
        + [sems, sems, sems, sems]
        + share_sems,
        compiler_params=pltpu.CompilerParams(
            collective_id=ident, has_side_effects=True, vmem_limit_bytes=60 * 1024 * 1024
        ),
        cost_estimate=pl.CostEstimate(flops=0, bytes_accessed=cost * MICROSECOND, transcendentals=0),
        name=f"scatter{ident}",
    )(*arrays)


def pack_gains(blocks, width):
    n = blocks[0].shape[0]
    rows = [jnp.pad(block, ((0, 0), (0, width - block.shape[1]))) for block in blocks]
    packed = jnp.stack(rows, axis=1)
    return jnp.pad(packed, ((0, 0), (0, SUBLANES - len(blocks)), (0, 0)))


def local(
    n_dp,
    n_tensor,
    hidden,
    in_gain,
    w_query,
    w_key,
    w_value,
    query_gain,
    key_gain,
    w_output,
    attn_gain,
    ffn_gain,
    w_gate,
    w_up,
    w_down,
    out_gain,
    cotangent,
    segment_ids,
    positions,
):
    factor = HD ** (-0.5)
    gains = (in_gain, attn_gain, ffn_gain, out_gain, query_gain, key_gain)
    width = -(-max(gain.shape[0] for gain in gains) // LANES) * LANES
    gain_rows = pack_gains([gain[None] for gain in gains], width)[0]
    attn_full = gather(
        "dp", n_dp, [gain_rows, w_query, w_key, w_value, w_output.T], 1, 0, 36
    )
    full_in_gain, full_attn_gain, full_ffn_gain, full_out_gain, full_qgain, full_kgain = (
        attn_full[0][:, row, : gain.shape[0]].reshape(-1) for row, gain in enumerate(gains)
    )
    full_query, full_key, full_value, full_output = (
        block.reshape(-1, block.shape[-1]) for block in attn_full[1:]
    )
    heads_local = full_query.shape[1] // HD
    hidden_f = hidden.astype(jnp.float32)
    normed_local = apply_norm(hidden_f, full_in_gain).astype(jnp.bfloat16)
    normed_in = gather("tensor", n_tensor, [normed_local], 5, 2, 13)[0].reshape(-1, normed_local.shape[-1])
    seq_len = normed_in.shape[0]
    query_raw = jnp.dot(normed_in, full_query, preferred_element_type=jnp.float32).reshape(
        seq_len, heads_local, HD
    )
    key_raw = jnp.dot(normed_in, full_key, preferred_element_type=jnp.float32)
    value_rows = jnp.dot(normed_in, full_value, preferred_element_type=jnp.float32).astype(
        jnp.bfloat16
    )
    cosine, sine_table = rotary_tables(positions, HD)
    query_rot = rotate(
        apply_norm(query_raw, full_qgain), cosine[:, None, :], sine_table[:, None, :]
    ).astype(jnp.bfloat16)
    key_rot = rotate(apply_norm(key_raw, full_kgain), cosine, sine_table).astype(jnp.bfloat16)
    allowed = window_mask(segment_ids)[None]
    scores = (
        jnp.einsum("qhd,kd->hqk", query_rot, key_rot, preferred_element_type=jnp.float32) * factor
    )
    log_total = jnp.log(jnp.sum(jnp.where(allowed, jnp.exp(scores), 0.0), axis=-1, keepdims=True))
    probs_low = jnp.where(allowed, jnp.exp(scores - log_total), 0.0).astype(jnp.bfloat16)
    context = jnp.einsum("hqk,kd->qhd", probs_low, value_rows, preferred_element_type=jnp.float32)
    context = context.reshape(seq_len, heads_local * HD).astype(jnp.bfloat16)
    attn_part = contract_cols(context, full_output)
    attn_rows = scatter(
        "tensor",
        n_tensor,
        [attn_part.astype(jnp.bfloat16).reshape(n_tensor, -1, attn_part.shape[-1])],
        5,
        6,
        14,
    )[0]
    residual = hidden_f + apply_norm(attn_rows, full_attn_gain)
    full_gate = lax.all_gather(w_gate, "dp", axis=0, tiled=True)
    full_up = lax.all_gather(w_up, "dp", axis=0, tiled=True)
    full_down = gather("dp", n_dp, [w_down.T], 9, 1, 55)[0].reshape(-1, w_down.shape[0])
    ffn_local = apply_norm(residual, full_ffn_gain).astype(jnp.bfloat16)
    ffn_in = gather("tensor", n_tensor, [ffn_local], 5, 3, 13)[0].reshape(-1, ffn_local.shape[-1])
    gate_pre = jnp.dot(ffn_in, full_gate, preferred_element_type=jnp.float32)
    up_pre = jnp.dot(ffn_in, full_up, preferred_element_type=jnp.float32)
    gelu_values, gelu_back = jax.vjp(gelu_tanh, gate_pre)
    mixed = (gelu_values * up_pre).astype(jnp.bfloat16)
    down_part = contract_cols(mixed, full_down)
    down_rows = scatter(
        "tensor",
        n_tensor,
        [down_part.astype(jnp.bfloat16).reshape(n_tensor, -1, down_part.shape[-1])],
        5,
        7,
        14,
    )[0]
    output = (residual + apply_norm(down_rows, full_out_gain)).astype(jnp.bfloat16)
    cot_f = cotangent.astype(jnp.float32)
    grad_down, term_out = norm_back(down_rows, full_out_gain, cot_f)
    down_all = gather("tensor", n_tensor, [grad_down.astype(jnp.bfloat16)], 5, 4, 13)[0].reshape(-1, grad_down.shape[-1])
    grad_wd = contract_rows(down_all, mixed)
    grad_mixed = jnp.dot(down_all, full_down, preferred_element_type=jnp.float32)
    gate_low = gelu_back(grad_mixed * up_pre)[0].astype(jnp.bfloat16)
    up_low = (grad_mixed * gelu_values).astype(jnp.bfloat16)
    grad_wg = contract_rows(ffn_in, gate_low)
    grad_wu = contract_rows(ffn_in, up_low)
    ffn_part = contract_cols(gate_low, full_gate) + contract_cols(up_low, full_up)
    ffn_back = scatter(
        "tensor",
        n_tensor,
        [ffn_part.astype(jnp.bfloat16).reshape(n_tensor, -1, ffn_part.shape[-1])],
        5,
        8,
        14,
    )[0]
    resid_norm, term_ffn = norm_back(residual, full_ffn_gain, ffn_back)
    grad_residual = cot_f + resid_norm
    grad_attn, term_attn = norm_back(attn_rows, full_attn_gain, grad_residual)
    attn_all = gather("tensor", n_tensor, [grad_attn.astype(jnp.bfloat16)], 5, 5, 13)[0].reshape(-1, grad_attn.shape[-1])
    grad_wo = contract_rows(attn_all, context)
    grad_context = (
        jnp.dot(attn_all, full_output, preferred_element_type=jnp.float32)
        .astype(jnp.bfloat16)
        .reshape(seq_len, heads_local, HD)
    )
    scores_again = (
        jnp.einsum("qhd,kd->hqk", query_rot, key_rot, preferred_element_type=jnp.float32) * factor
    )
    probs = jnp.where(allowed, jnp.exp(scores_again - log_total), 0.0)
    grad_probs = jnp.einsum(
        "qhd,kd->hqk", grad_context, value_rows, preferred_element_type=jnp.float32
    )
    delta = jnp.sum(probs * grad_probs, axis=-1, keepdims=True)
    grad_scores = (probs * (grad_probs - delta) * factor).astype(jnp.bfloat16)
    value_heads = jnp.einsum(
        "hqk,qhd->khd", probs.astype(jnp.bfloat16), grad_context, preferred_element_type=jnp.float32
    ).astype(jnp.bfloat16)
    grad_qrot = jnp.einsum("hqk,kd->qhd", grad_scores, key_rot, preferred_element_type=jnp.float32)
    grad_kheads = jnp.einsum(
        "hqk,qhd->khd", grad_scores, query_rot, preferred_element_type=jnp.float32
    )
    grad_qraw, term_qgain = norm_back(
        query_raw, full_qgain, rotate(grad_qrot, cosine[:, None, :], -sine_table[:, None, :])
    )
    grad_kraw, term_kgain = norm_back(
        key_raw[:, None, :],
        full_kgain,
        rotate(grad_kheads, cosine[:, None, :], -sine_table[:, None, :]),
    )
    query_low = grad_qraw.astype(jnp.bfloat16).reshape(seq_len, heads_local * HD)
    key_low = grad_kraw.astype(jnp.bfloat16)
    grad_wq = contract_rows(normed_in, query_low)
    grad_wk = jnp.einsum("sd,she->de", normed_in, key_low, preferred_element_type=jnp.float32)
    grad_wv = jnp.einsum("sd,she->de", normed_in, value_heads, preferred_element_type=jnp.float32)
    attn_in_part = contract_cols(query_low, full_query)
    attn_in_part = attn_in_part + jnp.einsum(
        "she,de->sd", key_low, full_key, preferred_element_type=jnp.float32
    )
    attn_in_part = attn_in_part + jnp.einsum(
        "she,de->sd", value_heads, full_value, preferred_element_type=jnp.float32
    )
    attn_back = scatter(
        "tensor",
        n_tensor,
        [attn_in_part.astype(jnp.bfloat16).reshape(n_tensor, -1, attn_in_part.shape[-1])],
        5,
        9,
        14,
    )[0]
    in_norm, term_in = norm_back(hidden_f, full_in_gain, attn_back)
    grad_hidden = grad_residual + in_norm
    def blocks(values):
        return values.astype(jnp.bfloat16).reshape(n_dp, -1, values.shape[-1])

    own_gate, own_down = (
        lax.psum_scatter(
            grad.astype(jnp.bfloat16), "dp", scatter_dimension=0, tiled=True
        ).astype(jnp.float32)
        for grad in (grad_wg, grad_wd)
    )
    gain_grads = [
        jnp.sum(term, axis=tuple(range(term.ndim - 1))).astype(jnp.bfloat16).reshape(n_dp, -1)
        for term in (term_in, term_attn, term_ffn, term_out, term_qgain, term_kgain)
    ]
    attn_grads = scatter(
        "dp",
        n_dp,
        [
            blocks(grad_wk),
            blocks(grad_wv),
            pack_gains(gain_grads, width),
            blocks(grad_wq),
            blocks(grad_wo),
            blocks(grad_wu),
        ],
        3,
        11,
        100,
        shared=(0, 1, 2),
        other="tensor",
        n_other=n_tensor,
    )
    own_in, own_attn, own_ffn, own_out, own_q, own_k = (
        attn_grads[2][row, : gain.shape[0]] for row, gain in enumerate(gains)
    )
    return (
        output,
        grad_hidden,
        own_in,
        attn_grads[3],
        attn_grads[0],
        attn_grads[1],
        own_q,
        own_k,
        attn_grads[4].T,
        own_attn,
        own_ffn,
        own_gate,
        attn_grads[5],
        own_down.T,
        own_out,
    )


def solution(mesh):
    placed = (
        P(("dp", "tensor"), None),
        P("dp"),
        P("dp", "tensor"),
        P("dp", None),
        P("dp", None),
        P("dp"),
        P("dp"),
        P("tensor", "dp"),
        P("dp"),
        P("dp"),
        P("dp", "tensor"),
        P("dp", "tensor"),
        P("tensor", "dp"),
        P("dp"),
        P(("dp", "tensor"), None),
        P("dp"),
        P("dp"),
    )
    return jax.shard_map(
        functools.partial(local, mesh.shape["dp"], mesh.shape["tensor"]),
        mesh=mesh,
        in_specs=placed,
        out_specs=(
            P(("dp", "tensor"), None),
            P(("dp", "tensor"), None),
            P("dp"),
            P("dp", "tensor"),
            P("dp", None),
            P("dp", None),
            P("dp"),
            P("dp"),
            P("tensor", "dp"),
            P("dp"),
            P("dp"),
            P("dp", "tensor"),
            P("dp", "tensor"),
            P("tensor", "dp"),
            P("dp"),
        ),
        check_vma=False,
    )
```
